32 devices in a mesh: ctx: 4 (over z), head: 4 (over y, x), dp: 2 (over core).
Axes of the slice: x: 2, y: 2, z: 4, core: 2. Of those that a mesh axis runs over, the one named last changes fastest.
Arguments:
- query: bfloat16 [2, 1024, 4096], P('dp', 'ctx', 'head'), may hold values from -4 to 4
- out_grad: bfloat16 [2, 1024, 4096], P('dp', 'ctx', 'head'), may hold values from -6 to 6
- row_lse: float32 [2, 32, 1024], P('dp', 'head', 'ctx'), may hold values from 6 to 8
- row_delta: float32 [2, 32, 1024], P('dp', 'head', 'ctx'), may hold values from -72 to 72
- key_value: bfloat16 [2, 1024, 1024], P('dp', 'ctx', 'head'), may hold values from -9 to 9
- kv_grad_in: float32 [2, 1024, 1024], P('dp', 'ctx', 'head'), may hold values from -1.8 to 1.8
- layer_input: bfloat16 [2, 1024, 8192], P('dp', 'ctx', 'head'), may hold values from -0.119628906 to 0.119628906
- slot_order: int32 [8], replicated, may hold values from 0 to 7, each once
Outputs:
- q_grad: float32 [2, 1024, 4096], P('dp', 'ctx', 'head')
- kv_grad: float32 [2, 1024, 1024], P('dp', 'ctx', 'head')
- v_weight_grad: float32 [4, 2048, 512], P('head', ('ctx', 'dp'))
The draws below stay inside these ranges and needn't reach their ends.
Inputs may be any that keep to these rules, and one draw needn't show every extreme that they name: `slot_order`: A permutation of the slots: every part of 128 tokens of the sequence sits in exactly one slot; device i of ctx holds slots 2i and 2i+1.
All inputs are finite; a program needn't handle non-finite values.
Results may differ from the reference program's by a relative error of at most 0.0037.
Values may be sent and summed in bfloat16 or wider, within the bound.
No kernel may reach another device: no remote copies, remote signals or barrier semaphores. Data moves between devices by JAX's collectives and lax.ppermute only.
A program may use at most 64 MiB of HBM per device.

```python
import math
import jax
import jax.numpy as jnp
from jax import lax

DH = 128
HQ = 8
D_WIN = 8192
S_DEV = 256
TOKENS = 1024
SEQS = 2
N_SLOTS = 8
QHEADS = 32
N_CTX = 4
N_HEAD = 4


def with_spikes(values, rng, source, target, shards_of, factor):
    def block_of(dim):
        return (jnp.arange(values.shape[dim]) // (values.shape[dim] // shards_of)).reshape((-1,) + (1,) * (values.ndim - 1 - dim))

    near = jax.random.permutation(rng, shards_of)[block_of(target)]
    second = (block_of(target) + shards_of // 2) % shards_of
    return jnp.where((block_of(source) == near) | (block_of(source) == second), factor * values, values)


def level_of(rng, shape, shards, least, high):
    loudness, own = 1.0, jax.random.fold_in(rng, 6)
    for position, blocks in shards:
        draws = jnp.exp(jax.random.uniform(jax.random.fold_in(own, position), (blocks,), jnp.float32, least / len(shards), high / len(shards)))
        loudness = loudness * jnp.repeat(draws, shape[position] // blocks).reshape([-1 if axis == position else 1 for axis in range(len(shape))])
    return loudness


def bell_draw(rng, shape, deviation, bound, cuts=(), kind=jnp.bfloat16):
    values = deviation * jax.random.normal(rng, shape, jnp.float32)
    if cuts:
        values = values * level_of(rng, shape, cuts, -0.22, 0.18)
    return jnp.clip(values, -bound, bound).astype(kind)


def heavy_noise(stream_key, shape, width, reach, shards, heavy, kind=jnp.bfloat16):
    array = width * jax.random.normal(stream_key, shape, jnp.float32)
    if shards:
        array = array * level_of(stream_key, shape, shards, -0.22, 0.18)
    return jnp.clip(with_spikes(array, jax.random.fold_in(stream_key, 3), *heavy), -reach, reach).astype(kind)


def setup_inputs(seed: int = 0) -> dict:
    streams_of = jax.random.split(jax.random.key(seed), 9)
    query = bell_draw(streams_of[0], (SEQS, TOKENS, QHEADS * DH), 1.0, 4.0, ((0, 2), (1, 4), (2, 4)))
    out_grad = bell_draw(streams_of[1], (SEQS, TOKENS, QHEADS * DH), 1.0, 6.0, ((0, 2), (1, 4), (2, 4)))
    row_lse = jnp.clip(6.0 + 2.0 * jax.random.uniform(streams_of[2], (SEQS, QHEADS, TOKENS), jnp.float32) ** level_of(streams_of[2], (SEQS, QHEADS, TOKENS), ((0, 2), (1, 4), (2, 4)), -0.2, 0.2), 6.0, 8.0)
    row_delta = bell_draw(streams_of[3], (SEQS, QHEADS, TOKENS), 12.0, 72.0, ((0, 2), (1, 4), (2, 4)), jnp.float32)
    key_value = bell_draw(streams_of[4], (SEQS, TOKENS, N_HEAD * 2 * DH), 1.5, 9.0, ((0, 2), (1, 4), (2, 4)))
    kv_grad_in = bell_draw(streams_of[5], (SEQS, TOKENS, N_HEAD * 2 * DH), 0.3, 1.8, ((0, 2), (1, 4), (2, 4)), jnp.float32)
    layer_input = heavy_noise(streams_of[6], (SEQS, TOKENS, D_WIN), 0.02, 0.119628906, ((0, 2), (1, 4), (2, 4)), (1, 2, 4, 2.0))
    slot_order = jax.random.permutation(streams_of[7], N_SLOTS).astype(jnp.int32)
    return {"query": query, "out_grad": out_grad, "row_lse": row_lse, "row_delta": row_delta, "key_value": key_value, "kv_grad_in": kv_grad_in, "layer_input": layer_input, "slot_order": slot_order}


def pair_grads(query_blk, dout_blk, lse_blk, delta_blk, key_rows, value_rows, query_pos, key_pos, softmax_scale):
    query_f = query_blk.astype(jnp.float32)
    dout_f = dout_blk.astype(jnp.float32)
    key_f = key_rows.astype(jnp.float32)
    value_f = value_rows.astype(jnp.float32)
    scores = jnp.einsum('qhd,kd->hqk', query_f, key_f) * softmax_scale
    visible = key_pos[None, None, :] <= query_pos[None, :, None]
    weights = jnp.exp(jnp.where(visible, scores - lse_blk[:, :, None], -1e+30))
    weights_low = weights.astype(jnp.bfloat16)
    value_dots = jnp.einsum('qhd,kd->hqk', dout_f, value_f)
    score_grad = (weights * (value_dots - delta_blk[:, :, None])).astype(jnp.bfloat16)
    score_f = score_grad.astype(jnp.float32)
    query_grad = jnp.einsum('hqk,kd->qhd', score_f, key_f) * softmax_scale
    key_grad = jnp.einsum('hqk,qhd->kd', score_f, query_f) * softmax_scale
    value_part = jnp.einsum('hqk,qhd->kd', weights_low.astype(jnp.float32), dout_f)
    return (query_grad, key_grad, value_part)

def reference(query, out_grad, row_lse, row_delta, key_value, kv_grad_in, layer_input, slot_order):
    half_len = S_DEV // 2
    softmax_scale = 1.0 / math.sqrt(DH)
    positions = (slot_order.reshape(N_CTX, 2)[:, :, None] * half_len + jnp.arange(half_len, dtype=jnp.int32)[None, None, :]).reshape(N_CTX, S_DEV)
    query_out = []
    kv_out = []
    for seq_idx in range(SEQS):

        def one_head(head_idx):
            query_head = lax.dynamic_slice_in_dim(query[seq_idx], head_idx * HQ * DH, HQ * DH, 1).reshape(N_CTX, S_DEV, HQ, DH)
            dout_head = lax.dynamic_slice_in_dim(out_grad[seq_idx], head_idx * HQ * DH, HQ * DH, 1).reshape(N_CTX, S_DEV, HQ, DH)
            lse_head = lax.dynamic_slice_in_dim(row_lse[seq_idx], head_idx * HQ, HQ, 0).reshape(HQ, N_CTX, S_DEV)
            delta_head = lax.dynamic_slice_in_dim(row_delta[seq_idx], head_idx * HQ, HQ, 0).reshape(HQ, N_CTX, S_DEV)
            kv_head = lax.dynamic_slice_in_dim(key_value[seq_idx], head_idx * 2 * DH, 2 * DH, 1).reshape(N_CTX, S_DEV, 2 * DH)
            kvin_head = lax.dynamic_slice_in_dim(kv_grad_in[seq_idx], head_idx * 2 * DH, 2 * DH, 1).reshape(N_CTX, S_DEV, 2 * DH)

            def one_block(block_idx):
                left_block = (block_idx + N_CTX - 1) % N_CTX
                right_block = (block_idx + 1) % N_CTX
                kv_both = jnp.concatenate([kv_head[left_block], kv_head[right_block]], axis=0)
                key_pos = jnp.concatenate([positions[left_block], positions[right_block]], axis=0)
                query_grad, key_grad, value_part = pair_grads(query_head[block_idx], dout_head[block_idx], lse_head[:, block_idx], delta_head[:, block_idx], kv_both[:, :DH], kv_both[:, DH:], positions[block_idx], key_pos, softmax_scale)
                return (query_grad.reshape(S_DEV, HQ * DH), jnp.concatenate([key_grad, value_part], axis=1))
            query_all, partial_all = lax.map(one_block, jnp.arange(N_CTX, dtype=jnp.int32))
            to_left = partial_all[:, :S_DEV]
            to_right = partial_all[:, S_DEV:]
            kv_new = kvin_head + jnp.roll(to_left, -1, axis=0) + jnp.roll(to_right, 1, axis=0)
            return (query_all.reshape(TOKENS, HQ * DH), kv_new.reshape(TOKENS, 2 * DH))
        query_heads, kv_heads = lax.map(one_head, jnp.arange(N_HEAD, dtype=jnp.int32))
        query_out.append(jnp.transpose(query_heads, (1, 0, 2)).reshape(TOKENS, N_HEAD * HQ * DH))
        kv_out.append(jnp.transpose(kv_heads, (1, 0, 2)).reshape(TOKENS, N_HEAD * 2 * DH))
    q_grad = jnp.stack(query_out, axis=0)
    kv_grad = jnp.stack(kv_out, axis=0)
    value_grad = kv_grad.reshape(SEQS, TOKENS, N_HEAD, 2, DH)[:, :, :, 1, :].reshape(SEQS, TOKENS, N_HEAD * DH).astype(jnp.bfloat16)
    summed = jnp.zeros((D_WIN, N_HEAD * DH), jnp.float32)
    for seq_idx in range(SEQS):
        summed = summed + jnp.dot(layer_input[seq_idx].T, value_grad[seq_idx], preferred_element_type=jnp.float32)
    return (q_grad, kv_grad, summed.reshape(N_HEAD, D_WIN // N_HEAD, N_HEAD * DH))
```

```python
import functools
import math

import jax
import jax.numpy as jnp
from jax import lax
from jax.experimental import pallas as pl
from jax.experimental.pallas import tpu as pltpu
from jax.sharding import PartitionSpec as P


NT = (((1,), (1,)), ((), ()))
NN = (((1,), (0,)), ((), ()))


def shift(value, axis, steps):
    count = lax.axis_size(axis)
    return lax.ppermute(value, axis, [(i, (i + steps) % count) for i in range(count)])


def swap(value, axis, bits):
    count = lax.axis_size(axis)
    return lax.ppermute(value, axis, [(i, i ^ bits) for i in range(count)])


def dot(a, b, dims):
    return lax.dot_general(a, b, dims, preferred_element_type=jnp.float32)


def masked_lse(lse_row, slots_ref, place_ref, half, key_half):
    key_at = slots_ref[2 * place_ref[1 + key_half // 2] + key_half % 2]
    lane = lax.broadcasted_iota(jnp.int32, lse_row.shape, 1)
    own = jnp.where(lane < half, slots_ref[2 * place_ref[0]], slots_ref[2 * place_ref[0] + 1])
    return jnp.where(key_at < own, lse_row, lse_row + 1e30)


def value_kernel(slots_ref, place_ref, q_ref, g_ref, lse_ref, kl_ref, kr_ref, vl_ref, vr_ref, acc_ref, *, heads, dim, scale):
    half = q_ref.shape[0] // 2
    acc_ref[...] = jnp.zeros_like(acc_ref)

    def head(m, carry):
        cols = pl.ds(pl.multiple_of(m * dim, dim), dim)
        q = q_ref[:, cols]
        g = g_ref[:, cols]
        lse = lse_ref[pl.ds(m, 1), :]
        for kh in range(4):
            key_ref = kl_ref if kh < 2 else kr_ref
            rows = slice((kh % 2) * half, (kh % 2 + 1) * half)
            s = dot(key_ref[rows, :], q, NT)
            low = masked_lse(lse, slots_ref, place_ref, half, kh)
            p = jnp.exp(s * scale - low).astype(jnp.bfloat16)
            acc_ref[kh * half : (kh + 1) * half, :] += dot(p, g, NN)
        return carry

    lax.fori_loop(0, heads, head, 0)
    vl_ref[...] = acc_ref[: 2 * half, :].astype(vl_ref.dtype)
    vr_ref[...] = acc_ref[2 * half :, :].astype(vr_ref.dtype)


def query_kernel(
    slots_ref, place_ref, q_ref, g_ref, lse_ref, delta_ref, kl_ref, kr_ref, vl_ref, vr_ref,
    dq_ref, dl_ref, dr_ref, acc_ref, *, heads, dim, scale
):
    half = q_ref.shape[0] // 2
    acc_ref[...] = jnp.zeros_like(acc_ref)
    keys_t = jnp.concatenate([kl_ref[...].T, kr_ref[...].T], axis=1)

    def head(m, carry):
        cols = pl.ds(pl.multiple_of(m * dim, dim), dim)
        q = q_ref[:, cols]
        g = g_ref[:, cols]
        lse = lse_ref[pl.ds(m, 1), :]
        delta = delta_ref[pl.ds(m, 1), :]
        dq_t = jnp.zeros((dim, 2 * half), jnp.float32)
        for kh in range(4):
            key_ref = kl_ref if kh < 2 else kr_ref
            value_ref = vl_ref if kh < 2 else vr_ref
            rows = slice((kh % 2) * half, (kh % 2 + 1) * half)
            s = dot(key_ref[rows, :], q, NT)
            low = masked_lse(lse, slots_ref, place_ref, half, kh)
            p = jnp.exp(s * scale - low)
            dp = dot(value_ref[rows, :], g, NT)
            ds = (p * (dp - delta)).astype(jnp.bfloat16)
            acc_ref[kh * half : (kh + 1) * half, :] += dot(ds, q, NN)
            dq_t += dot(keys_t[:, kh * half : (kh + 1) * half], ds, NN)
        dq_ref[:, cols] = (dq_t * scale).T
        return carry

    lax.fori_loop(0, heads, head, 0)
    dl_ref[...] = (acc_ref[: 2 * half, :] * scale).astype(dl_ref.dtype)
    dr_ref[...] = (acc_ref[2 * half :, :] * scale).astype(dr_ref.dtype)


def on_device(query, out_grad, row_lse, row_delta, key_value, kv_grad_in, layer_input, slot_order):
    ctx_n = lax.axis_size("ctx")
    head_n = lax.axis_size("head")
    dp_n = lax.axis_size("dp")
    c = lax.axis_index("ctx")
    h = lax.axis_index("head")
    d = lax.axis_index("dp")
    tokens = query.shape[1]
    dim = key_value.shape[2] // 2
    heads = query.shape[2] // dim
    scale = 1.0 / math.sqrt(dim)
    bf16 = jnp.bfloat16
    smem = pl.BlockSpec(memory_space=pltpu.SMEM)
    vmem = pl.BlockSpec(memory_space=pltpu.VMEM)

    place = jnp.stack([c, (c + ctx_n - 1) % ctx_n, (c + 1) % ctx_n]).astype(jnp.int32)
    kv = key_value[0]
    keys = kv[:, :dim]
    values = kv[:, dim:]
    key_l = shift(keys, "ctx", 1)
    key_r = shift(keys, "ctx", -1)
    value_l = shift(values, "ctx", 1)
    value_r = shift(values, "ctx", -1)

    x = layer_input[0]
    rows = x.shape[1] // (ctx_n * dp_n)
    blocks = ctx_n // 2
    x5 = x.reshape(tokens, blocks, 2, dp_n, rows)

    def pick(i, j):
        part = lax.dynamic_slice(x5, (0, 0, i, j, 0), (tokens, blocks, 1, 1, rows))
        return part.reshape(tokens, blocks * rows)

    odd = c % 2
    x_own = pick(odd, d)
    x_ctx = swap(pick(1 - odd, d), "ctx", 1)
    x_dp = swap(pick(odd, 1 - d), "dp", 1)
    x_both = lax.ppermute(
        pick(1 - odd, 1 - d),
        ("ctx", "dp"),
        [(i * dp_n + j, (i ^ 1) * dp_n + (j ^ 1)) for i in range(ctx_n) for j in range(dp_n)],
    )

    q2 = query[0]
    g2 = out_grad[0]
    lse = row_lse[0]
    delta = row_delta[0]
    part = jax.ShapeDtypeStruct((tokens, dim), bf16)
    dv_l, dv_r = pl.pallas_call(
        functools.partial(value_kernel, heads=heads, dim=dim, scale=scale),
        out_shape=(part, part),
        in_specs=[smem, smem] + [vmem] * 5,
        out_specs=(vmem, vmem),
        scratch_shapes=[pltpu.VMEM((2 * tokens, dim), jnp.float32)],
        name="value_part",
    )(slot_order, place, q2, g2, lse, key_l, key_r)
    value_back_r = shift(dv_l, "ctx", -1)
    value_back_l = shift(dv_r, "ctx", 1)

    dq, dk_l, dk_r = pl.pallas_call(
        functools.partial(query_kernel, heads=heads, dim=dim, scale=scale),
        out_shape=(jax.ShapeDtypeStruct((tokens, heads * dim), jnp.float32), part, part),
        in_specs=[smem, smem] + [vmem] * 8,
        out_specs=(vmem,) * 3,
        scratch_shapes=[pltpu.VMEM((2 * tokens, dim), jnp.float32)],
        name="query_part",
    )(slot_order, place, q2, g2, lse, delta, key_l, key_r, value_l, value_r)
    key_back_r = shift(dk_l, "ctx", -1)
    key_back_l = shift(dk_r, "ctx", 1)

    kv_in = kv_grad_in[0]
    value_new = kv_in[:, dim:] + value_back_r.astype(jnp.float32) + value_back_l.astype(jnp.float32)
    key_new = kv_in[:, :dim] + key_back_r.astype(jnp.float32) + key_back_l.astype(jnp.float32)
    kv_grad = jnp.concatenate([key_new, value_new], axis=1)
    value_grad = value_new.astype(bf16)

    pair = jnp.concatenate([value_grad, swap(value_grad, "ctx", 1)], axis=0)
    own_seq = jnp.concatenate([pair] + [swap(pair, "head", s) for s in range(1, head_n)], axis=1)
    other_seq = swap(own_seq, "dp", 1)
    TN = (((0,), (0,)), ((), ()))
    partial = (
        dot(x_own, own_seq[:tokens], TN)
        + dot(x_ctx, own_seq[tokens:], TN)
        + dot(x_dp, other_seq[:tokens], TN)
        + dot(x_both, other_seq[tokens:], TN)
    )
    level = c // 2
    span = blocks
    while span > 1:
        span //= 2
        high = (level // span) % 2
        halves = partial.reshape(2, span * rows, partial.shape[1])
        keep = lax.dynamic_index_in_dim(halves, high, 0, keepdims=False)
        give = lax.dynamic_index_in_dim(halves, 1 - high, 0, keepdims=False).astype(bf16)
        partial = keep + swap(give, "ctx", 2 * span).astype(jnp.float32)
    cols = partial.reshape(rows, head_n, dim)
    order = jnp.arange(head_n, dtype=jnp.int32) ^ h
    weight = jnp.take(cols, order, axis=1).reshape(rows, head_n * dim)
    return (dq[None], kv_grad[None], weight[None])


def solution(mesh):
    in_specs = (
        P("dp", "ctx", "head"),
        P("dp", "ctx", "head"),
        P("dp", "head", "ctx"),
        P("dp", "head", "ctx"),
        P("dp", "ctx", "head"),
        P("dp", "ctx", "head"),
        P("dp", "ctx", "head"),
        P(),
    )
    out_specs = (P("dp", "ctx", "head"), P("dp", "ctx", "head"), P("head", ("ctx", "dp"), None))
    return jax.shard_map(
        on_device, mesh=mesh, in_specs=in_specs, out_specs=out_specs, check_vma=False
    )
```
